256 devices in a mesh: section: 16 (over y_hi, z), seq: 16 (over y_lo, x, core).
Axes of the slice: x: 4, y: 4 (y_hi: 2, y_lo: 2; y = y_hi * 2 + y_lo), z: 8, core: 2. Of those that a mesh axis runs over, the one named last changes fastest.
Arguments:
- stream: bfloat16 [16, 2048, 2048], P('section', 'seq'), may hold values from -6 to 6
- queries: bfloat16 [16, 2048, 2048], P('section', 'seq'), may hold values from -5 to 5
- key_rows: bfloat16 [16, 2048, 2048], P('section', 'seq'), may hold values from -5 to 5
- value_rows: bfloat16 [16, 2048, 2048], P('section', 'seq'), may hold values from -6 to 6
- o_weight: bfloat16 [16, 2048, 2048], P('section', 'seq'), may hold values from -0.125 to 0.125
- norm_gain: float32 [16, 2048], P('section'), may hold values from 0.1 to 1.9
- w_gate: bfloat16 [16, 2048, 7168], P('section', None, 'seq'), may hold values from -0.125 to 0.125
- w_up: bfloat16 [16, 2048, 7168], P('section', None, 'seq'), may hold values from -0.125 to 0.125
- w_down: bfloat16 [16, 7168, 2048], P('section', 'seq'), may hold values from -0.0625 to 0.0625
Outputs:
- passed: bfloat16 [16, 2048, 2048], P('section', 'seq')
The draws below stay inside these ranges and needn't reach their ends.
All inputs are finite; a program needn't handle non-finite values.
Results may differ from the reference program's by a relative error of at most 0.012.
Values may be sent and summed in bfloat16 or wider, within the bound.
No kernel may reach another device: no remote copies, remote signals or barrier semaphores. Data moves between devices by JAX's collectives and lax.ppermute only.
A program may use at most 64 MiB of HBM per device.

```python
import jax
import jax.numpy as jnp
from jax import lax

D = 2048
HEADS = 16
HEAD_DIM = 128
FFW = 7168
TOKENS = 2048
N_SECTION = 16
N_SEQ = 16


def base_draw(key):
    shape = (N_SECTION, TOKENS, HEADS * HEAD_DIM)
    return jnp.clip(jax.random.normal(key, shape, jnp.float32), -5.0, 5.0)


def draw_queries(key, part):
    base = base_draw(jax.random.fold_in(key, 21))
    return base.astype(jnp.bfloat16)


def draw_key_rows(key, part):
    base = base_draw(jax.random.fold_in(key, 22))
    return base.astype(jnp.bfloat16)


def block_levels(stream_key, shape, cuts, least, largest):
    level = 1.0
    for dim, blocks in cuts:
        heights = jax.random.uniform(jax.random.fold_in(jax.random.fold_in(stream_key, 6), dim), (blocks,), jnp.float32, least / len(cuts), largest / len(cuts))
        level = level * jnp.repeat(jnp.exp(heights), shape[dim] // blocks).reshape((-1,) + (1,) * (len(shape) - 1 - dim))
    return level


def scatter_about(key, dims, scale, bound, cuts=(), held_as=jnp.bfloat16):
    drawn = jax.random.normal(key, dims, jnp.float32) * scale
    if len(cuts) > 0:
        drawn = block_levels(key, dims, cuts, -0.22, 0.18) * drawn
    return jnp.clip(drawn, min=-bound, max=bound).astype(held_as)


def setup_inputs(seed: int = 0) -> dict:
    streams_of = jax.random.split(jax.random.key(seed), 10)
    stream = scatter_about(streams_of[0], (N_SECTION, TOKENS, D), 1.0, 6.0, ((0, 16), (1, 16)))
    queries = draw_queries(jax.random.fold_in(streams_of[9], 71), 0)
    key_rows = draw_key_rows(jax.random.fold_in(streams_of[9], 71), 0)
    value_rows = scatter_about(streams_of[3], (N_SECTION, TOKENS, HEADS * HEAD_DIM), 1.0, 6.0, ((0, 16), (1, 16)))
    o_weight = scatter_about(streams_of[4], (N_SECTION, HEADS * HEAD_DIM, D), (HEADS * HEAD_DIM) ** -0.5, 0.125, ((0, 16), (1, 16)))
    norm_gain = jnp.clip(1.0 + 0.18 * jax.random.normal(streams_of[5], (N_SECTION, D), jnp.float32), 0.1, 1.9)
    w_gate = scatter_about(streams_of[6], (N_SECTION, D, FFW), D ** -0.5, 0.125, ((0, 16), (2, 16)))
    w_up = scatter_about(streams_of[7], (N_SECTION, D, FFW), D ** -0.5, 0.125, ((0, 16), (2, 16)))
    w_down = scatter_about(streams_of[8], (N_SECTION, FFW, D), FFW ** -0.5, 0.0625, ((0, 16), (1, 16)))
    return dict(stream=stream, queries=queries, key_rows=key_rows, value_rows=value_rows, o_weight=o_weight, norm_gain=norm_gain, w_gate=w_gate, w_up=w_up, w_down=w_down)


def attend_head(pieces):
    query_head, key_head, value_head = pieces
    length = query_head.shape[0]
    scores = jnp.dot(query_head.astype(jnp.float32), key_head.astype(jnp.float32).T) * HEAD_DIM ** (-0.5)
    row_pos = lax.broadcasted_iota(jnp.int32, (length, length), 0)
    col_pos = lax.broadcasted_iota(jnp.int32, (length, length), 1)
    scores = jnp.where(col_pos <= row_pos, scores, -1e+30)
    highest = lax.optimization_barrier(jnp.max(scores, axis=-1, keepdims=True))
    powers = jnp.exp(scores - highest)
    weights = (powers / lax.optimization_barrier(jnp.sum(powers, axis=-1, keepdims=True))).astype(jnp.bfloat16)
    mixture = jnp.dot(weights.astype(jnp.float32), value_head.astype(jnp.float32))
    return mixture.astype(jnp.bfloat16)

def attend(queries, key_rows, value_rows):
    moved = (jnp.transpose(queries, (1, 0, 2)), jnp.transpose(key_rows, (1, 0, 2)), jnp.transpose(value_rows, (1, 0, 2)))
    mixed = lax.map(attend_head, moved)
    return jnp.transpose(mixed, (1, 0, 2))

def blocked_sum(left, right, blocks):
    block_width = left.shape[1] // blocks

    def add_block(block_index, running):
        offset = (jnp.asarray(block_index).astype(jnp.int32) * block_width).astype(jnp.int32)
        part_left = lax.dynamic_slice_in_dim(left, offset, block_width, 1)
        part_right = lax.dynamic_slice_in_dim(right, offset, block_width, 0)
        partial_value = jnp.dot(part_left, part_right, preferred_element_type=jnp.float32).astype(jnp.bfloat16)
        partial_value = lax.optimization_barrier(partial_value)
        return running + partial_value.astype(jnp.float32)
    return lax.fori_loop(0, blocks, add_block, jnp.zeros((left.shape[0], right.shape[1]), jnp.float32))

def one_section(pieces):
    stream, queries, key_rows, value_rows, o_weight, norm_gain, w_gate, w_up, w_down = pieces
    attended = attend(queries.reshape(TOKENS, HEADS, HEAD_DIM), key_rows.reshape(TOKENS, HEADS, HEAD_DIM), value_rows.reshape(TOKENS, HEADS, HEAD_DIM))
    attended = attended.reshape(TOKENS, HEADS * HEAD_DIM)
    residual = stream.astype(jnp.float32) + blocked_sum(attended, o_weight, N_SEQ)
    normed = (residual * lax.rsqrt(lax.optimization_barrier(jnp.mean(residual * residual, axis=-1, keepdims=True)) + 1e-05) * norm_gain).astype(jnp.bfloat16)
    gate_pre = jnp.dot(normed, w_gate, preferred_element_type=jnp.float32)
    up_pre = jnp.dot(normed, w_up, preferred_element_type=jnp.float32)
    hidden = (jax.nn.silu(gate_pre) * up_pre).astype(jnp.bfloat16)
    ffn_sum = blocked_sum(hidden, w_down, N_SEQ)
    return (residual + ffn_sum).astype(jnp.bfloat16)

def reference(stream, queries, key_rows, value_rows, o_weight, norm_gain, w_gate, w_up, w_down):
    results = lax.map(one_section, (stream, queries, key_rows, value_rows, o_weight, norm_gain, w_gate, w_up, w_down))
    return jnp.roll(results, 1, axis=0)
```

```python
import jax
import jax.numpy as jnp
import numpy as np
from jax import lax
from jax.experimental import pallas as pl
from jax.experimental.pallas import tpu as pltpu
from jax.sharding import Mesh, PartitionSpec as P

HEAD_DIM = 128
T = 128
D = 2048
SEQ = ("y", "x", "c")
BF = jnp.bfloat16
F32 = jnp.float32
VMEM = pl.BlockSpec(memory_space=pltpu.VMEM)
SMEM = pl.BlockSpec(memory_space=pltpu.SMEM)


def chip_shift(v, dy, dx):
    route = []
    for y in range(2):
        for x in range(4):
            route.append((y * 4 + x, ((y + dy) % 2) * 4 + (x + dx) % 4))
    return lax.ppermute(v, ("y", "x"), route)


def to_plus(v):
    return chip_shift(v, 0, 1)


def to_minus(v):
    return chip_shift(v, 0, -1)


def to_side(v):
    return chip_shift(v, 1, 0)


def to_core(v):
    return lax.ppermute(v, "c", [(0, 1), (1, 0)])


THIRDS = (0, 48, 96, 128)


def gather_rounds(own):
    m = to_plus(own)
    p = to_minus(own)
    s = to_side(own)
    first = {(0, 0): own, (0, -1): m, (0, 1): p, (1, 0): s}
    sm = to_plus(s)
    pp = to_minus(p)
    sp = to_side(p)
    second = {(1, -1): sm, (0, 2): pp, (1, 1): sp}
    a, b, c, d = THIRDS
    f0 = to_side(pp[a:b])
    f1 = to_minus(sp[b:c])
    f2 = to_plus(sm[c:d])
    third = {(1, 2): (f0, f1, f2)}
    return first, second, third


def pack_kernel(q, k, v, out):
    for j in range(16):
        cols = slice(j * HEAD_DIM, (j + 1) * HEAD_DIM)
        out[j, :, 0:128] = q[:, cols]
        out[j, :, 128:256] = k[:, cols]
        out[j, :, 256:384] = v[:, cols]


def pack(q, k, v):
    return pl.pallas_call(
        pack_kernel,
        out_shape=jax.ShapeDtypeStruct((16, T, 384), BF),
        in_specs=[VMEM] * 3,
        out_specs=VMEM,
        name="pack",
    )(q, k, v)


QB = 256


def attend_kernel(qkv, out):
    scale = HEAD_DIM ** -0.5
    row = lax.broadcasted_iota(jnp.int32, (QB, QB), 0)
    col = lax.broadcasted_iota(jnp.int32, (QB, QB), 1)
    keep = col <= row
    for i in range(2048 // QB):
        lo, hi = i * QB, (i + 1) * QB
        q = qkv[lo:hi, 0:128]
        dims = (((1,), (1,)), ((), ()))
        sd = lax.dot_general(q, qkv[lo:hi, 128:256], dims, preferred_element_type=F32) * scale
        sd = jnp.where(keep, sd, -1e30)
        top = jnp.max(sd, axis=-1, keepdims=True)
        if i > 0:
            sl = lax.dot_general(q, qkv[0:lo, 128:256], dims, preferred_element_type=F32) * scale
            top = jnp.maximum(top, jnp.max(sl, axis=-1, keepdims=True))
        ed = jnp.exp(sd - top)
        total = jnp.sum(ed, axis=-1, keepdims=True)
        mix = jnp.dot(ed.astype(BF), qkv[lo:hi, 256:384], preferred_element_type=F32)
        if i > 0:
            el = jnp.exp(sl - top)
            total = total + jnp.sum(el, axis=-1, keepdims=True)
            mix = mix + jnp.dot(el.astype(BF), qkv[0:lo, 256:384], preferred_element_type=F32)
        out[lo:hi, :] = (mix / total).astype(BF)


def attend(qkv):
    return pl.pallas_call(
        attend_kernel,
        out_shape=jax.ShapeDtypeStruct((2048, HEAD_DIM), BF),
        in_specs=[VMEM],
        out_specs=VMEM,
        cost_estimate=pl.CostEstimate(flops=1_200_000_000, bytes_accessed=2_097_152, transcendentals=2_400_000),
        name="attend",
    )(qkv)


def project_kernel(place, att, stream, gain, *refs):
    weights, (resid, normed, left) = refs[:-3], refs[-3:]
    for k in range(16):
        left[:, k * 128 : (k + 1) * 128] = att[place[k]]
    acc = stream[...].astype(F32)
    row = 0
    for w in weights:
        acc = acc + jnp.dot(left[:, row : row + w.shape[0]], w[...], preferred_element_type=F32)
        row += w.shape[0]
    resid[...] = acc
    mean = jnp.mean(acc * acc, axis=-1, keepdims=True)
    normed[...] = (acc * lax.rsqrt(mean + 1e-5) * gain[...]).astype(BF)


def project(place, att, stream, gain, weights):
    return pl.pallas_call(
        project_kernel,
        out_shape=(jax.ShapeDtypeStruct((T, D), F32), jax.ShapeDtypeStruct((T, D), BF)),
        in_specs=[SMEM] + [VMEM] * (3 + len(weights)),
        out_specs=(VMEM, VMEM),
        scratch_shapes=[pltpu.VMEM((T, D), BF)],
        cost_estimate=pl.CostEstimate(flops=1_100_000_000, bytes_accessed=10_000_000, transcendentals=128),
        name="project",
    )(place, att, stream, gain, *weights)


def ffn_kernel(count, *refs):
    shards = refs[:count]
    g0, g1, u0, u1, d0, d1 = refs[count : count + 6]
    outs = refs[count + 6 :]

    def hidden(v, g, u):
        gate = jnp.dot(v, g[...], preferred_element_type=F32)
        up = jnp.dot(v, u[...], preferred_element_type=F32)
        return (gate / (1.0 + jnp.exp(-gate)) * up).astype(BF)

    for v, o in zip(shards, outs):
        x = v[...]
        acc = jnp.dot(hidden(x, g0, u0), d0[...], preferred_element_type=F32)
        acc = acc + jnp.dot(hidden(x, g1, u1), d1[...], preferred_element_type=F32)
        o[...] = acc.astype(BF)


def ffn(shards, weights):
    n = len(shards)
    tokens = sum(s.shape[0] for s in shards)
    outs = pl.pallas_call(
        lambda *refs: ffn_kernel(n, *refs),
        out_shape=tuple(jax.ShapeDtypeStruct(s.shape, BF) for s in shards),
        in_specs=[VMEM] * (n + 6),
        out_specs=(VMEM,) * n,
        cost_estimate=pl.CostEstimate(
            flops=6 * tokens * 2048 * 896, bytes_accessed=11_000_000 + tokens * 8192, transcendentals=tokens * 896
        ),
        name="ffn",
    )(*shards, *weights)
    return outs


def added(*vs):
    acc = vs[0].astype(F32)
    for v in vs[1:]:
        acc = acc + v.astype(F32)
    return acc.astype(BF)


def shards(stream, queries, key_rows, value_rows, o_weight, norm_gain, w_gate, w_up, w_down):
    y, x, c = (lax.axis_index(n) for n in SEQ)
    weights = []
    for w in (w_gate[0], w_up[0], w_down[0]):
        weights += [w, to_core(w)]

    packed = pack(queries[0], key_rows[0], value_rows[0])
    qkv = lax.all_to_all(packed, SEQ, split_axis=0, concat_axis=0, tiled=True)

    first, second, third = gather_rounds(o_weight[0])
    order, pieces = [], []
    for group in (first, second, third):
        for (dy, dx), w in group.items():
            order.append(((y + dy) % 2) * 4 + (x + dx) % 4)
            pieces.append(w)
    flat = []
    for w in pieces:
        flat += list(w) if isinstance(w, tuple) else [w]
    flat = [jnp.concatenate(flat[0:4], 0), jnp.concatenate(flat[4:7], 0), jnp.concatenate(flat[7:], 0)]
    flat = flat + [to_core(w) for w in flat]
    place = jnp.stack([2 * o + c for o in order] + [2 * o + 1 - c for o in order]).astype(jnp.int32)

    attended = attend(qkv.reshape(2048, 384))
    returned = lax.all_to_all(attended.reshape(16, T, HEAD_DIM), SEQ, split_axis=0, concat_axis=0, tiled=True)
    residual, normed = project(place, returned, stream[0], norm_gain, flat)

    first, second, third = gather_rounds(normed)
    far = jnp.concatenate(third[(1, 2)], 0)
    own_, m_, p_, s_ = ffn(list(first.values()), weights)
    sm_, pp_, sp_ = ffn(list(second.values()), weights)
    (far_,) = ffn([far], weights)

    a, b, cc, d = THIRDS
    r0 = to_side(far_[a:b])
    r1 = to_plus(far_[b:cc])
    r2 = to_minus(far_[cc:d])
    pp_ = jnp.concatenate([added(pp_[a:b], r0), pp_[b:]], 0)
    sp_ = jnp.concatenate([sp_[:b], added(sp_[b:cc], r1), sp_[cc:]], 0)
    sm_ = jnp.concatenate([sm_[:cc], added(sm_[cc:], r2)], 0)
    t0 = to_minus(sm_)
    t1 = to_plus(pp_)
    t2 = to_side(sp_)
    s_ = added(s_, t0)
    p_ = added(p_, t1, t2)
    v0 = to_minus(m_)
    v1 = to_plus(p_)
    v2 = to_side(s_)
    finished = (
        residual + own_.astype(F32) + v0.astype(F32) + v1.astype(F32) + v2.astype(F32)
    ).astype(BF)
    passed = lax.ppermute(finished, "s", [((i - 1) % 16, i) for i in range(16)])
    return passed[None]


def solution(mesh):
    fine = Mesh(np.asarray(mesh.devices).reshape(16, 2, 4, 2), ("s", "y", "x", "c"))
    rows = P("s", SEQ, None)
    placed = (rows, rows, rows, rows, rows, P("s", None), P("s", None, SEQ), P("s", None, SEQ), rows)
    return jax.shard_map(shards, mesh=fine, in_specs=placed, out_specs=rows, check_vma=False)
```

```python
import jax
import jax.numpy as jnp
import numpy as np
from jax import lax
from jax.experimental import pallas as pl
from jax.experimental.pallas import tpu as pltpu
from jax.sharding import Mesh, PartitionSpec as P

HEAD_DIM = 128
T = 128
D = 2048
SEQ = ("y", "x", "c")
BF = jnp.bfloat16
F32 = jnp.float32
VMEM = pl.BlockSpec(memory_space=pltpu.VMEM)
MB = 1 << 20
HBM = pl.BlockSpec(memory_space=pltpu.MemorySpace.HBM)
ANY = pl.BlockSpec(memory_space=pl.ANY)
SMEM = pl.BlockSpec(memory_space=pltpu.SMEM)


def chip_shift(v, dy, dx):
    route = []
    for y in range(2):
        for x in range(4):
            route.append((y * 4 + x, ((y + dy) % 2) * 4 + (x + dx) % 4))
    return lax.ppermute(v, ("y", "x"), route)


def to_plus(v):
    return chip_shift(v, 0, 1)


def to_minus(v):
    return chip_shift(v, 0, -1)


def to_side(v):
    return chip_shift(v, 1, 0)


def to_core(v):
    return lax.ppermute(v, "c", [(0, 1), (1, 0)])


THIRDS = (0, 48, 96, 128)


FIRST = ((0, 0), (0, -1), (0, 1), (1, 0))
SECOND = ((1, -1), (0, 2), (1, 1))


def gather_first(own):
    return {(0, 0): own, (0, -1): to_plus(own), (0, 1): to_minus(own), (1, 0): to_side(own)}


def gather_second(first):
    p, s = first[0, 1], first[1, 0]
    return {(1, -1): to_plus(s), (0, 2): to_minus(p), (1, 1): to_side(p)}


def gather_third(second):
    a, b, c, d = THIRDS
    return (to_side(second[0, 2][a:b]), to_minus(second[1, 1][b:c]), to_plus(second[1, -1][c:d]))


def pack_kernel(q, k, v, out, held, sem):
    copies = [pltpu.make_async_copy(ref, held.at[n], sem.at[n]) for n, ref in enumerate((q, k, v))]
    for copy in copies:
        copy.start()
    for n, copy in enumerate(copies):
        copy.wait()
        for j in range(16):
            out[j, :, n * 128 : (n + 1) * 128] = held[n, :, j * HEAD_DIM : (j + 1) * HEAD_DIM]


def pack(q, k, v):
    return pl.pallas_call(
        pack_kernel,
        out_shape=jax.ShapeDtypeStruct((16, T, 384), BF),
        in_specs=[HBM] * 3,
        out_specs=VMEM,
        scratch_shapes=[pltpu.VMEM((3, T, D), BF), pltpu.SemaphoreType.DMA((3,))],
        compiler_params=pltpu.CompilerParams(vmem_limit_bytes=8 * MB),
        name="pack",
    )(q, k, v)


QB = 256


def attend_kernel(qkv, out):
    scale = HEAD_DIM ** -0.5
    row = lax.broadcasted_iota(jnp.int32, (QB, QB), 0)
    col = lax.broadcasted_iota(jnp.int32, (QB, QB), 1)
    keep = col <= row
    for i in range(2048 // QB):
        lo, hi = i * QB, (i + 1) * QB
        q = qkv[lo:hi, 0:128]
        dims = (((1,), (1,)), ((), ()))
        sd = lax.dot_general(q, qkv[lo:hi, 128:256], dims, preferred_element_type=F32) * scale
        sd = jnp.where(keep, sd, -1e30)
        top = jnp.max(sd, axis=-1, keepdims=True)
        if i > 0:
            sl = lax.dot_general(q, qkv[0:lo, 128:256], dims, preferred_element_type=F32) * scale
            top = jnp.maximum(top, jnp.max(sl, axis=-1, keepdims=True))
        ed = jnp.exp(sd - top)
        total = jnp.sum(ed, axis=-1, keepdims=True)
        mix = jnp.dot(ed.astype(BF), qkv[lo:hi, 256:384], preferred_element_type=F32)
        if i > 0:
            el = jnp.exp(sl - top)
            total = total + jnp.sum(el, axis=-1, keepdims=True)
            mix = mix + jnp.dot(el.astype(BF), qkv[0:lo, 256:384], preferred_element_type=F32)
        out[lo:hi, :] = (mix / total).astype(BF)


def attend(qkv):
    return pl.pallas_call(
        attend_kernel,
        out_shape=jax.ShapeDtypeStruct((2048, HEAD_DIM), BF),
        in_specs=[VMEM],
        out_specs=VMEM,
        cost_estimate=pl.CostEstimate(flops=1_200_000_000, bytes_accessed=2_097_152, transcendentals=2_400_000),
        compiler_params=pltpu.CompilerParams(vmem_limit_bytes=28 * MB),
        name="attend",
    )(qkv)


CHUNK = 512


def project_kernel(place, att, stream, gain, *refs):
    weights, (resid, normed, left, held, sem) = refs[:-5], refs[-5:]
    copies, row = [], 0
    for w in weights:
        copies.append((row, pltpu.make_async_copy(w, held.at[pl.ds(row, w.shape[0]), :], sem.at[len(copies)])))
        row += w.shape[0]
    for _, copy in copies:
        copy.start()
    for k in range(16):
        left[:, k * 128 : (k + 1) * 128] = att[place[k]]
    acc = stream[...].astype(F32)
    for lo in range(0, 2048, CHUNK):
        for at, copy in copies:
            if lo <= at < lo + CHUNK:
                copy.wait()
        acc = acc + jnp.dot(left[:, lo : lo + CHUNK], held[lo : lo + CHUNK, :], preferred_element_type=F32)
    resid[...] = acc
    mean = jnp.mean(acc * acc, axis=-1, keepdims=True)
    normed[...] = (acc * lax.rsqrt(mean + 1e-5) * gain[...]).astype(BF)


def project(place, att, stream, gain, weights):
    return pl.pallas_call(
        project_kernel,
        out_shape=(jax.ShapeDtypeStruct((T, D), F32), jax.ShapeDtypeStruct((T, D), BF)),
        in_specs=[SMEM] + [VMEM] * 3 + [ANY] * len(weights),
        out_specs=(VMEM, VMEM),
        scratch_shapes=[
            pltpu.VMEM((T, D), BF),
            pltpu.VMEM((2048, D), BF),
            pltpu.SemaphoreType.DMA((len(weights),)),
        ],
        cost_estimate=pl.CostEstimate(flops=1_100_000_000, bytes_accessed=10_000_000, transcendentals=128),
        compiler_params=pltpu.CompilerParams(vmem_limit_bytes=20 * MB),
        name="project",
    )(place, att, stream, gain, *weights)


NT = (((1,), (1,)), ((), ()))


def ffn_kernel(count, *refs):
    shards = refs[:count]
    weights = refs[count : count + 6]
    outs = refs[count + 6 : 2 * count + 6]
    x, acc = refs[2 * count + 6 :]
    row = 0
    for v in shards:
        x[row : row + v.shape[0], :] = v[...]
        row += v.shape[0]
    for part in range(2):
        g, u, d = weights[part * 3 : part * 3 + 3]
        gate = lax.dot_general(x[...], g[...], NT, preferred_element_type=F32)
        gate = gate / (1.0 + jnp.exp(-gate))
        up = lax.dot_general(x[...], u[...], NT, preferred_element_type=F32)
        hidden = (gate * up).astype(BF)
        share = jnp.dot(hidden, d[...], preferred_element_type=F32)
        if part == 0:
            acc[...] = share
        else:
            row = 0
            for o in outs:
                n = o.shape[0]
                o[...] = (acc[row : row + n, :] + share[row : row + n, :]).astype(BF)
                row += n


def ffn(shards, weights):
    n = len(shards)
    tokens = sum(s.shape[0] for s in shards)
    outs = pl.pallas_call(
        lambda *refs: ffn_kernel(n, *refs),
        out_shape=tuple(jax.ShapeDtypeStruct(s.shape, BF) for s in shards),
        in_specs=[VMEM] * (n + 6),
        out_specs=(VMEM,) * n,
        scratch_shapes=[pltpu.VMEM((tokens, D), BF), pltpu.VMEM((tokens, D), F32)],
        cost_estimate=pl.CostEstimate(
            flops=6 * tokens * 2048 * 896, bytes_accessed=11_000_000 + tokens * 8192, transcendentals=tokens * 896
        ),
        compiler_params=pltpu.CompilerParams(vmem_limit_bytes=30 * MB),
        name="ffn",
    )(*shards, *weights)
    return outs


def merge_kernel(pp, sp, sm, r0, r1, r2, pp_out, sp_out, sm_out):
    a, b, c, d = THIRDS
    for ref, r, out, lo, hi in ((pp, r0, pp_out, a, b), (sp, r1, sp_out, b, c), (sm, r2, sm_out, c, d)):
        out[...] = ref[...]
        out[lo:hi, :] = (ref[lo:hi, :].astype(F32) + r[...].astype(F32)).astype(BF)


def merge(*vs):
    return pl.pallas_call(
        merge_kernel,
        out_shape=(jax.ShapeDtypeStruct((T, D), BF),) * 3,
        in_specs=[VMEM] * 6,
        out_specs=(VMEM,) * 3,
        compiler_params=pltpu.CompilerParams(vmem_limit_bytes=10 * MB),
        name="merge",
    )(*vs)


def added(*vs):
    acc = vs[0].astype(F32)
    for v in vs[1:]:
        acc = acc + v.astype(F32)
    return acc.astype(BF)


def layer(stream, queries, key_rows, value_rows, o_weight, norm_gain, w_gate, w_up, w_down):
    y, x, c = (lax.axis_index(n) for n in SEQ)
    first = gather_first(o_weight[0])
    packed = pack(queries[0], key_rows[0], value_rows[0])
    qkv = lax.all_to_all(packed, SEQ, split_axis=0, concat_axis=0, tiled=True)
    mine = (w_gate[0].T, w_up[0].T, w_down[0])
    weights = list(mine) + [to_core(w) for w in mine]
    second = gather_second(first)
    attended = attend(qkv.reshape(2048, 384))
    returned = lax.all_to_all(attended.reshape(16, T, HEAD_DIM), SEQ, split_axis=0, concat_axis=0, tiled=True)
    pieces = [first[k] for k in FIRST] + [second[k] for k in SECOND]
    pieces += list(gather_third(second))
    pieces += [to_core(w) for w in pieces]
    order = [((y + dy) % 2) * 4 + (x + dx) % 4 for dy, dx in FIRST + SECOND + ((1, 2),)]
    place = jnp.stack([2 * o + c for o in order] + [2 * o + 1 - c for o in order]).astype(jnp.int32)
    residual, normed = project(place, returned, stream[0], norm_gain, pieces)

    first = gather_first(normed)
    second = gather_second(first)
    outs = ffn([first[k] for k in FIRST], weights)
    outs, second = lax.optimization_barrier((outs, second))
    own_, m_, p_, s_ = outs
    far = ffn(list(gather_third(second)), weights)
    far, second = lax.optimization_barrier((far, [second[k] for k in SECOND]))
    r0 = to_side(far[0])
    r1 = to_plus(far[1])
    r2 = to_minus(far[2])
    sm_, pp_, sp_ = ffn(second, weights)
    pp_, sp_, sm_ = merge(pp_, sp_, sm_, r0, r1, r2)
    t0 = to_minus(sm_)
    t1 = to_plus(pp_)
    t2 = to_side(sp_)
    s_ = added(s_, t0)
    p_ = added(p_, t1, t2)
    v0 = to_minus(m_)
    v1 = to_plus(p_)
    v2 = to_side(s_)
    finished = (
        residual + own_.astype(F32) + v0.astype(F32) + v1.astype(F32) + v2.astype(F32)
    ).astype(BF)
    passed = lax.ppermute(finished, "s", [((i - 1) % 16, i) for i in range(16)])
    return passed[None]


def solution(mesh):
    fine = Mesh(np.asarray(mesh.devices).reshape(16, 2, 4, 2), ("s", "y", "x", "c"))
    rows = P("s", SEQ, None)
    placed = (rows, rows, rows, rows, rows, P("s", None), P("s", None, SEQ), P("s", None, SEQ), rows)
    return jax.shard_map(layer, mesh=fine, in_specs=placed, out_specs=rows, check_vma=False)
```

```python
import jax
import jax.numpy as jnp
import numpy as np
from jax import lax
from jax.experimental import pallas as pl
from jax.experimental.pallas import tpu as pltpu
from jax.sharding import Mesh, PartitionSpec as P

HEAD_DIM = 128
T = 128
D = 2048
SEQ = ("y", "x", "c")
BF = jnp.bfloat16
F32 = jnp.float32
VMEM = pl.BlockSpec(memory_space=pltpu.VMEM)
MB = 1 << 20
HBM = pl.BlockSpec(memory_space=pltpu.MemorySpace.HBM)
ANY = pl.BlockSpec(memory_space=pl.ANY)
SMEM = pl.BlockSpec(memory_space=pltpu.SMEM)


def chip_shift(v, dy, dx):
    route = []
    for y in range(2):
        for x in range(4):
            route.append((y * 4 + x, ((y + dy) % 2) * 4 + (x + dx) % 4))
    return lax.ppermute(v, ("y", "x"), route)


def to_plus(v):
    return chip_shift(v, 0, 1)


def to_minus(v):
    return chip_shift(v, 0, -1)


def to_side(v):
    return chip_shift(v, 1, 0)


def to_core(v):
    return lax.ppermute(v, "c", [(0, 1), (1, 0)])


THIRDS = (0, 48, 96, 128)


FIRST = ((0, 0), (0, -1), (0, 1), (1, 0))
SECOND = ((1, -1), (0, 2), (1, 1))


def gather_first(own):
    return {(0, 0): own, (0, -1): to_plus(own), (0, 1): to_minus(own), (1, 0): to_side(own)}


def gather_second(first):
    p, s = first[0, 1], first[1, 0]
    return {(1, -1): to_plus(s), (0, 2): to_minus(p), (1, 1): to_side(p)}


def gather_third(second):
    a, b, c, d = THIRDS
    return (to_side(second[0, 2][a:b]), to_minus(second[1, 1][b:c]), to_plus(second[1, -1][c:d]))


def pack_kernel(q, k, v, out, held, sem):
    copies = [pltpu.make_async_copy(ref, held.at[n], sem.at[n]) for n, ref in enumerate((q, k, v))]
    for copy in copies:
        copy.start()
    for n, copy in enumerate(copies):
        copy.wait()
        for j in range(16):
            out[j, :, n * 128 : (n + 1) * 128] = held[n, :, j * HEAD_DIM : (j + 1) * HEAD_DIM]


def pack(q, k, v):
    return pl.pallas_call(
        pack_kernel,
        out_shape=jax.ShapeDtypeStruct((16, T, 384), BF),
        in_specs=[HBM] * 3,
        out_specs=VMEM,
        scratch_shapes=[pltpu.VMEM((3, T, D), BF), pltpu.SemaphoreType.DMA((3,))],
        name="pack",
    )(q, k, v)


QB = 256
SPAN = 1024


def attend_kernel(qkv, out):
    scale = HEAD_DIM ** -0.5
    row = lax.broadcasted_iota(jnp.int32, (QB, SPAN), 0)
    col = lax.broadcasted_iota(jnp.int32, (QB, SPAN), 1)
    dims = (((1,), (1,)), ((), ()))
    for lo in range(0, 2048, SPAN):
        hi = lo + SPAN

        def block(j, carry, lo=lo, hi=hi):
            rows = pl.ds(lo + j * QB, QB)
            q = qkv[rows, 0:128]
            sd = lax.dot_general(q, qkv[lo:hi, 128:256], dims, preferred_element_type=F32) * scale
            sd = jnp.where(col <= row + j * QB, sd, -1e30)
            top = jnp.max(sd, axis=-1, keepdims=True)
            if lo > 0:
                sl = lax.dot_general(q, qkv[0:lo, 128:256], dims, preferred_element_type=F32) * scale
                top = jnp.maximum(top, jnp.max(sl, axis=-1, keepdims=True))
            ed = jnp.exp(sd - top)
            total = jnp.sum(ed, axis=-1, keepdims=True)
            mix = jnp.dot(ed.astype(BF), qkv[lo:hi, 256:384], preferred_element_type=F32)
            if lo > 0:
                el = jnp.exp(sl - top)
                total = total + jnp.sum(el, axis=-1, keepdims=True)
                mix = mix + jnp.dot(el.astype(BF), qkv[0:lo, 256:384], preferred_element_type=F32)
            out[rows, :] = (mix / total).astype(BF)
            return carry

        lax.fori_loop(0, SPAN // QB, block, 0)


def attend(qkv):
    return pl.pallas_call(
        attend_kernel,
        out_shape=jax.ShapeDtypeStruct((2048, HEAD_DIM), BF),
        in_specs=[VMEM],
        out_specs=VMEM,
        cost_estimate=pl.CostEstimate(flops=1_200_000_000, bytes_accessed=2_097_152, transcendentals=2_400_000),
        compiler_params=pltpu.CompilerParams(vmem_limit_bytes=28 * MB),
        name="attend",
    )(qkv)


CHUNK = 512


def project_kernel(place, att, *refs):
    weights, (mine, theirs, left, held, acc, sem) = refs[:-6], refs[-6:]
    copies, row = [], 0
    for w in weights:
        copies.append((row, pltpu.make_async_copy(w, held.at[pl.ds(row, w.shape[0]), :], sem.at[len(copies)])))
        row += w.shape[0]
    for _, copy in copies:
        copy.start()
    core = place[8]
    for k in range(8):
        left[0:T, k * 128 : (k + 1) * 128] = att[place[k], pl.ds(core * T, T), :]
        left[T : 2 * T, k * 128 : (k + 1) * 128] = att[place[k], pl.ds((1 - core) * T, T), :]
    for lo in range(0, 1024, CHUNK):
        for at, copy in copies:
            if lo <= at < lo + CHUNK:
                copy.wait()

        def columns(n, carry, lo=lo):
            cols = pl.ds(n * CHUNK, CHUNK)
            part = jnp.dot(left[:, lo : lo + CHUNK], held[lo : lo + CHUNK, cols], preferred_element_type=F32)
            if lo == 0:
                acc[:, cols] = part
            else:
                acc[:, cols] += part
            return carry

        lax.fori_loop(0, D // CHUNK, columns, 0)
    mine[...] = acc[0:T, :]
    theirs[...] = acc[T : 2 * T, :].astype(BF)


def project(place, att, weights):
    return pl.pallas_call(
        project_kernel,
        out_shape=(jax.ShapeDtypeStruct((T, D), F32), jax.ShapeDtypeStruct((T, D), BF)),
        in_specs=[SMEM, VMEM] + [ANY] * len(weights),
        out_specs=(VMEM,) * 2,
        scratch_shapes=[
            pltpu.VMEM((2 * T, 1024), BF),
            pltpu.VMEM((1024, D), BF),
            pltpu.VMEM((2 * T, D), F32),
            pltpu.SemaphoreType.DMA((len(weights),)),
        ],
        cost_estimate=pl.CostEstimate(flops=1_100_000_000, bytes_accessed=6_000_000, transcendentals=0),
        compiler_params=pltpu.CompilerParams(vmem_limit_bytes=20 * MB),
        name="project",
    )(place, att, *weights)


def norm_kernel(mine, other, stream, gain, resid, normed):
    acc = stream[...].astype(F32) + mine[...] + other[...].astype(F32)
    resid[...] = acc
    mean = jnp.mean(acc * acc, axis=-1, keepdims=True)
    normed[...] = (acc * lax.rsqrt(mean + 1e-5) * gain[...]).astype(BF)


def norm(mine, other, stream, gain):
    return pl.pallas_call(
        norm_kernel,
        out_shape=(jax.ShapeDtypeStruct((T, D), F32), jax.ShapeDtypeStruct((T, D), BF)),
        in_specs=[VMEM] * 4,
        out_specs=(VMEM,) * 2,
        compiler_params=pltpu.CompilerParams(vmem_limit_bytes=8 * MB),
        name="norm",
    )(mine, other, stream, gain)


def stack_kernel(axis, *refs):
    parts, out, sem = refs[:-2], refs[-2], refs[-1]
    copies = []
    for n, part in enumerate(parts):
        place = out.at[n] if axis == 0 else out.at[:, n]
        copies.append(pltpu.make_async_copy(part, place, sem.at[n]))
    for copy in copies:
        copy.start()
    for copy in copies:
        copy.wait()


def stack(parts, axis, space):
    n = len(parts)
    shape = parts[0].shape[:axis] + (n,) + parts[0].shape[axis:]
    return pl.pallas_call(
        lambda *refs: stack_kernel(axis, *refs),
        out_shape=jax.ShapeDtypeStruct(shape, BF),
        in_specs=[ANY] * n,
        out_specs=space,
        scratch_shapes=[pltpu.SemaphoreType.DMA((n,))],
        compiler_params=pltpu.CompilerParams(vmem_limit_bytes=14 * MB),
        name="stack",
    )(*parts)


NT = (((1,), (1,)), ((), ()))


def ffn_kernel(count, *refs):
    shards, weights, outs = refs[:count], refs[count], refs[count + 1 : -2]
    x, acc = refs[-2:]
    row = 0
    for v in shards:
        x[row : row + v.shape[0], :] = v[...]
        row += v.shape[0]

    block = min(x.shape[0], 128) if x.shape[0] == 512 else x.shape[0]

    def step(i, carry):
        part = i % 2
        rows = pl.ds((i // 2) * block, block)
        gate = lax.dot_general(x[rows, :], weights[0, part], NT, preferred_element_type=F32)
        gate = gate / (1.0 + jnp.exp(-gate))
        up = lax.dot_general(x[rows, :], weights[1, part], NT, preferred_element_type=F32)
        hidden = (gate * up).astype(BF)
        share = jnp.dot(hidden, weights[2, part], preferred_element_type=F32)
        acc[rows, :] = jnp.where(part == 0, 0.0, acc[rows, :]) + share
        return carry

    lax.fori_loop(0, 2 * (x.shape[0] // block), step, 0)
    row = 0
    for o in outs:
        o[...] = acc[row : row + o.shape[0], :].astype(BF)
        row += o.shape[0]


def ffn(shards, weights, sizes=None):
    n = len(shards)
    sizes = sizes or [v.shape[0] for v in shards]
    tokens = sum(sizes)
    return pl.pallas_call(
        lambda *refs: ffn_kernel(n, *refs),
        out_shape=tuple(jax.ShapeDtypeStruct((size, D), BF) for size in sizes),
        in_specs=[VMEM] * (n + 1),
        out_specs=(VMEM,) * len(sizes),
        scratch_shapes=[pltpu.VMEM((tokens, D), BF), pltpu.VMEM((tokens, D), F32)],
        cost_estimate=pl.CostEstimate(
            flops=6 * tokens * 2048 * 896, bytes_accessed=tokens * 8192, transcendentals=tokens * 896
        ),
        compiler_params=pltpu.CompilerParams(vmem_limit_bytes=24 * MB),
        name="ffn",
    )(*shards, weights)


SPLIT = 2
H = T // SPLIT


def merge_kernel(*refs):
    pieces, returned, outs = refs[0:3], refs[3:6], refs[6:]
    for n in range(3):
        lo, hi = THIRDS[n], THIRDS[n + 1]
        for h in range(SPLIT):
            out, start = outs[SPLIT * n + h], h * H
            out[...] = pieces[n][start : start + H, :]
            a, b = max(lo, start), min(hi, start + H)
            if a < b:
                both = pieces[n][a:b, :].astype(F32) + returned[n][a - lo : b - lo, :].astype(F32)
                out[a - start : b - start, :] = both.astype(BF)


def merge(pieces, returned):
    return pl.pallas_call(
        merge_kernel,
        out_shape=(jax.ShapeDtypeStruct((H, D), BF),) * (3 * SPLIT),
        in_specs=[VMEM] * 6,
        out_specs=(VMEM,) * (3 * SPLIT),
        compiler_params=pltpu.CompilerParams(vmem_limit_bytes=10 * MB),
        name="merge",
    )(*pieces, *returned)


def finish_kernel(start, residual, own, v0, v1, v2, out):
    total = residual[start : start + H, :] + own[...].astype(F32)
    for v in (v0, v1, v2):
        total = total + v[...].astype(F32)
    out[...] = total.astype(BF)


def finish(start, *vs):
    return pl.pallas_call(
        lambda *refs: finish_kernel(start, *refs),
        out_shape=jax.ShapeDtypeStruct((H, D), BF),
        in_specs=[VMEM] * 5,
        out_specs=VMEM,
        compiler_params=pltpu.CompilerParams(vmem_limit_bytes=6 * MB),
        name="finish",
    )(*vs)


def added(*vs):
    acc = vs[0].astype(F32)
    for v in vs[1:]:
        acc = acc + v.astype(F32)
    return acc.astype(BF)


def layer(stream, queries, key_rows, value_rows, o_weight, norm_gain, w_gate, w_up, w_down):
    y, x, c = (lax.axis_index(n) for n in SEQ)
    first = gather_first(o_weight[0])
    packed = pack(queries[0], key_rows[0], value_rows[0])
    qkv = lax.all_to_all(packed, SEQ, split_axis=0, concat_axis=0, tiled=True)
    own = stack((w_gate[0].T, w_up[0].T, w_down[0]), 0, ANY)
    across = to_core(own)
    weights = stack((own, across), 1, VMEM)
    second = gather_second(first)
    attended = attend(qkv.reshape(2048, 384))
    blocks = attended.reshape(8, 2 * T, HEAD_DIM)
    returned = lax.all_to_all(blocks, ("y", "x"), split_axis=0, concat_axis=0, tiled=True)
    pieces = [first[k] for k in FIRST] + [second[k] for k in SECOND]
    pieces += list(gather_third(second))
    order = [((y + dy) % 2) * 4 + (x + dx) % 4 for dy, dx in FIRST + SECOND + ((1, 2),)]
    place = jnp.stack(order + [c]).astype(jnp.int32)
    mine, theirs = project(place, returned, pieces)
    residual, normed = norm(mine, to_core(theirs), stream[0], norm_gain)

    first = gather_first(normed)
    second = gather_second(first)
    outs = ffn([first[k] for k in FIRST], weights, [H] * (4 * SPLIT))
    outs, second = lax.optimization_barrier((outs, second))
    far = ffn(list(gather_third(second)), weights)
    far, second = lax.optimization_barrier((far, [second[k] for k in SECOND]))
    r0 = to_side(far[0])
    r1 = to_plus(far[1])
    r2 = to_minus(far[2])
    sm_, pp_, sp_ = ffn(second, weights)
    merged = merge((pp_, sp_, sm_), (r0, r1, r2))
    shares = []
    for h in range(SPLIT):
        pp_, sp_, sm_ = merged[h::SPLIT]
        shares.append((to_minus(sm_), to_plus(pp_), to_side(sp_)))
    done = []
    for h in range(SPLIT):
        t0, t1, t2 = shares[h]
        own_, m_, p_, s_ = outs[h::SPLIT]
        s_ = added(s_, t0)
        p_ = added(p_, t1, t2)
        arrived = to_minus(m_), to_plus(p_), to_side(s_)
        total = finish(h * H, residual, own_, *arrived)
        done.append(lax.ppermute(total, "s", [((i - 1) % 16, i) for i in range(16)]))
    return jnp.concatenate(done, 0)[None]


def solution(mesh):
    fine = Mesh(np.asarray(mesh.devices).reshape(16, 2, 4, 2), ("s", "y", "x", "c"))
    rows = P("s", SEQ, None)
    placed = (rows, rows, rows, rows, rows, P("s", None), P("s", None, SEQ), P("s", None, SEQ), rows)
    return jax.shard_map(layer, mesh=fine, in_specs=placed, out_specs=rows, check_vma=False)
```

```python
import jax
import jax.numpy as jnp
import numpy as np
from jax import lax
from jax.experimental import pallas as pl
from jax.experimental.pallas import tpu as pltpu
from jax.sharding import Mesh, PartitionSpec as P

HEAD_DIM = 128
T = 128
D = 2048
SEQ = ("y", "x", "c")
BF = jnp.bfloat16
F32 = jnp.float32
VMEM = pl.BlockSpec(memory_space=pltpu.VMEM)
MB = 1 << 20
HBM = pl.BlockSpec(memory_space=pltpu.MemorySpace.HBM)
ANY = pl.BlockSpec(memory_space=pl.ANY)
SMEM = pl.BlockSpec(memory_space=pltpu.SMEM)


def chip_shift(v, dy, dx):
    route = []
    for y in range(2):
        for x in range(4):
            route.append((y * 4 + x, ((y + dy) % 2) * 4 + (x + dx) % 4))
    return lax.ppermute(v, ("y", "x"), route)


def to_plus(v):
    return chip_shift(v, 0, 1)


def to_minus(v):
    return chip_shift(v, 0, -1)


def to_side(v):
    return chip_shift(v, 1, 0)


def to_core(v):
    return lax.ppermute(v, "c", [(0, 1), (1, 0)])


THIRDS = (0, 48, 96, 128)


FIRST = ((0, 0), (0, -1), (0, 1), (1, 0))
SECOND = ((1, -1), (0, 2), (1, 1))


def gather_first(own):
    return {(0, 0): own, (0, -1): to_plus(own), (0, 1): to_minus(own), (1, 0): to_side(own)}


def gather_second(first):
    p, s = first[0, 1], first[1, 0]
    return {(1, -1): to_plus(s), (0, 2): to_minus(p), (1, 1): to_side(p)}


def gather_third(second):
    a, b, c, d = THIRDS
    return (to_side(second[0, 2][a:b]), to_minus(second[1, 1][b:c]), to_plus(second[1, -1][c:d]))


def pack_kernel(q, k, v, out, held, sem):
    copies = [pltpu.make_async_copy(ref, held.at[n], sem.at[n]) for n, ref in enumerate((q, k, v))]
    for copy in copies:
        copy.start()
    for n, copy in enumerate(copies):
        copy.wait()
        for j in range(16):
            out[j, :, n * 128 : (n + 1) * 128] = held[n, :, j * HEAD_DIM : (j + 1) * HEAD_DIM]


def pack(q, k, v):
    return pl.pallas_call(
        pack_kernel,
        out_shape=jax.ShapeDtypeStruct((16, T, 384), BF),
        in_specs=[HBM] * 3,
        out_specs=VMEM,
        scratch_shapes=[pltpu.VMEM((3, T, D), BF), pltpu.SemaphoreType.DMA((3,))],
        name="pack",
    )(q, k, v)


QB = 256
SPAN = 1024


def attend_kernel(qkv, out):
    rate = HEAD_DIM ** -0.5 * 1.4426950408889634
    row = lax.broadcasted_iota(jnp.int32, (QB, SPAN), 0)
    col = lax.broadcasted_iota(jnp.int32, (QB, SPAN), 1)
    dims = (((1,), (1,)), ((), ()))
    for lo in range(0, 2048, SPAN):
        hi = lo + SPAN

        def block(j, carry, lo=lo, hi=hi):
            rows = pl.ds(lo + j * QB, QB)
            q = qkv[rows, 0:128]
            sd = lax.dot_general(q, qkv[lo:hi, 128:256], dims, preferred_element_type=F32)
            sd = jnp.where(col <= row + j * QB, sd, -1e30)
            top = jnp.max(sd, axis=-1, keepdims=True)
            if lo > 0:
                sl = lax.dot_general(q, qkv[0:lo, 128:256], dims, preferred_element_type=F32)
                top = jnp.maximum(top, jnp.max(sl, axis=-1, keepdims=True))
            ed = jnp.exp2((sd - top) * rate)
            total = jnp.sum(ed, axis=-1, keepdims=True)
            mix = jnp.dot(ed.astype(BF), qkv[lo:hi, 256:384], preferred_element_type=F32)
            if lo > 0:
                el = jnp.exp2((sl - top) * rate)
                total = total + jnp.sum(el, axis=-1, keepdims=True)
                mix = mix + jnp.dot(el.astype(BF), qkv[0:lo, 256:384], preferred_element_type=F32)
            out[rows, :] = (mix / total).astype(BF)
            return carry

        lax.fori_loop(0, SPAN // QB, block, 0)


def attend(qkv):
    return pl.pallas_call(
        attend_kernel,
        out_shape=jax.ShapeDtypeStruct((2048, HEAD_DIM), BF),
        in_specs=[VMEM],
        out_specs=VMEM,
        cost_estimate=pl.CostEstimate(flops=1_200_000_000, bytes_accessed=2_097_152, transcendentals=2_400_000),
        compiler_params=pltpu.CompilerParams(vmem_limit_bytes=28 * MB),
        name="attend",
    )(qkv)


CHUNK = 512


def project_kernel(place, att, *refs):
    weights, (mine, theirs, left, held, acc, sem) = refs[:-6], refs[-6:]
    copies, row = [], 0
    for w in weights:
        copies.append((row, pltpu.make_async_copy(w, held.at[pl.ds(row, w.shape[0]), :], sem.at[len(copies)])))
        row += w.shape[0]
    for _, copy in copies:
        copy.start()
    core = place[8]
    for k in range(8):
        left[0:T, k * 128 : (k + 1) * 128] = att[place[k], pl.ds(core * T, T), :]
        left[T : 2 * T, k * 128 : (k + 1) * 128] = att[place[k], pl.ds((1 - core) * T, T), :]
    for lo in range(0, 1024, CHUNK):
        for at, copy in copies:
            if lo <= at < lo + CHUNK:
                copy.wait()

        def columns(n, carry, lo=lo):
            cols = pl.ds(n * CHUNK, CHUNK)
            part = jnp.dot(left[:, lo : lo + CHUNK], held[lo : lo + CHUNK, cols], preferred_element_type=F32)
            if lo == 0:
                acc[:, cols] = part
            else:
                acc[:, cols] += part
            return carry

        lax.fori_loop(0, D // CHUNK, columns, 0)
    mine[...] = acc[0:T, :]
    theirs[...] = acc[T : 2 * T, :].astype(BF)


def project(place, att, weights):
    return pl.pallas_call(
        project_kernel,
        out_shape=(jax.ShapeDtypeStruct((T, D), F32), jax.ShapeDtypeStruct((T, D), BF)),
        in_specs=[SMEM, VMEM] + [ANY] * len(weights),
        out_specs=(VMEM,) * 2,
        scratch_shapes=[
            pltpu.VMEM((2 * T, 1024), BF),
            pltpu.VMEM((1024, D), BF),
            pltpu.VMEM((2 * T, D), F32),
            pltpu.SemaphoreType.DMA((len(weights),)),
        ],
        cost_estimate=pl.CostEstimate(flops=1_100_000_000, bytes_accessed=6_000_000, transcendentals=0),
        compiler_params=pltpu.CompilerParams(vmem_limit_bytes=20 * MB),
        name="project",
    )(place, att, *weights)


def norm_kernel(mine, other, stream, gain, resid, normed):
    acc = stream[...].astype(F32) + mine[...] + other[...].astype(F32)
    resid[...] = acc
    mean = jnp.mean(acc * acc, axis=-1, keepdims=True)
    normed[...] = (acc * lax.rsqrt(mean + 1e-5) * gain[...]).astype(BF)


def norm(mine, other, stream, gain):
    return pl.pallas_call(
        norm_kernel,
        out_shape=(jax.ShapeDtypeStruct((T, D), F32), jax.ShapeDtypeStruct((T, D), BF)),
        in_specs=[VMEM] * 4,
        out_specs=(VMEM,) * 2,
        compiler_params=pltpu.CompilerParams(vmem_limit_bytes=8 * MB),
        name="norm",
    )(mine, other, stream, gain)


def stack_kernel(axis, *refs):
    parts, out, sem = refs[:-2], refs[-2], refs[-1]
    copies = []
    for n, part in enumerate(parts):
        place = out.at[n] if axis == 0 else out.at[:, n]
        copies.append(pltpu.make_async_copy(part, place, sem.at[n]))
    for copy in copies:
        copy.start()
    for copy in copies:
        copy.wait()


def stack(parts, axis, space):
    n = len(parts)
    shape = parts[0].shape[:axis] + (n,) + parts[0].shape[axis:]
    return pl.pallas_call(
        lambda *refs: stack_kernel(axis, *refs),
        out_shape=jax.ShapeDtypeStruct(shape, BF),
        in_specs=[ANY] * n,
        out_specs=space,
        scratch_shapes=[pltpu.SemaphoreType.DMA((n,))],
        compiler_params=pltpu.CompilerParams(vmem_limit_bytes=14 * MB),
        name="stack",
    )(*parts)


NT = (((1,), (1,)), ((), ()))


def ffn_kernel(count, *refs):
    shards, weights, outs = refs[:count], refs[count], refs[count + 1 : -2]
    x, acc = refs[-2:]
    row = 0
    for v in shards:
        x[row : row + v.shape[0], :] = v[...]
        row += v.shape[0]

    block = min(x.shape[0], 256) if x.shape[0] == 512 else x.shape[0]

    def step(i, carry):
        part = i % 2
        rows = pl.ds((i // 2) * block, block)
        gate = lax.dot_general(x[rows, :], weights[0, part], NT, preferred_element_type=F32)
        gate = gate / (1.0 + jnp.exp(-gate))
        up = lax.dot_general(x[rows, :], weights[1, part], NT, preferred_element_type=F32)
        hidden = (gate * up).astype(BF)
        share = jnp.dot(hidden, weights[2, part], preferred_element_type=F32)
        acc[rows, :] = jnp.where(part == 0, 0.0, acc[rows, :]) + share
        return carry

    lax.fori_loop(0, 2 * (x.shape[0] // block), step, 0)
    row = 0
    for o in outs:
        o[...] = acc[row : row + o.shape[0], :].astype(BF)
        row += o.shape[0]


def ffn(shards, weights, sizes=None):
    n = len(shards)
    sizes = sizes or [v.shape[0] for v in shards]
    tokens = sum(sizes)
    return pl.pallas_call(
        lambda *refs: ffn_kernel(n, *refs),
        out_shape=tuple(jax.ShapeDtypeStruct((size, D), BF) for size in sizes),
        in_specs=[VMEM] * (n + 1),
        out_specs=(VMEM,) * len(sizes),
        scratch_shapes=[pltpu.VMEM((tokens, D), BF), pltpu.VMEM((tokens, D), F32)],
        cost_estimate=pl.CostEstimate(
            flops=6 * tokens * 2048 * 896, bytes_accessed=tokens * 8192, transcendentals=tokens * 896
        ),
        compiler_params=pltpu.CompilerParams(vmem_limit_bytes=24 * MB),
        name="ffn",
    )(*shards, weights)


SPLIT = 2
H = T // SPLIT


def merge_kernel(*refs):
    pieces, returned, outs = refs[0:3], refs[3:6], refs[6:]
    for n in range(3):
        lo, hi = THIRDS[n], THIRDS[n + 1]
        for h in range(SPLIT):
            out, start = outs[SPLIT * n + h], h * H
            out[...] = pieces[n][start : start + H, :]
            a, b = max(lo, start), min(hi, start + H)
            if a < b:
                both = pieces[n][a:b, :].astype(F32) + returned[n][a - lo : b - lo, :].astype(F32)
                out[a - start : b - start, :] = both.astype(BF)


def merge(pieces, returned):
    return pl.pallas_call(
        merge_kernel,
        out_shape=(jax.ShapeDtypeStruct((H, D), BF),) * (3 * SPLIT),
        in_specs=[VMEM] * 6,
        out_specs=(VMEM,) * (3 * SPLIT),
        compiler_params=pltpu.CompilerParams(vmem_limit_bytes=10 * MB),
        name="merge",
    )(*pieces, *returned)


def finish_kernel(start, residual, own, v0, v1, v2, out):
    total = residual[start : start + H, :] + own[...].astype(F32)
    for v in (v0, v1, v2):
        total = total + v[...].astype(F32)
    out[...] = total.astype(BF)


def finish(start, *vs):
    return pl.pallas_call(
        lambda *refs: finish_kernel(start, *refs),
        out_shape=jax.ShapeDtypeStruct((H, D), BF),
        in_specs=[VMEM] * 5,
        out_specs=VMEM,
        compiler_params=pltpu.CompilerParams(vmem_limit_bytes=6 * MB),
        name="finish",
    )(*vs)


def added(*vs):
    acc = vs[0].astype(F32)
    for v in vs[1:]:
        acc = acc + v.astype(F32)
    return acc.astype(BF)


def layer(stream, queries, key_rows, value_rows, o_weight, norm_gain, w_gate, w_up, w_down):
    y, x, c = (lax.axis_index(n) for n in SEQ)
    first = gather_first(o_weight[0])
    packed = pack(queries[0], key_rows[0], value_rows[0])
    qkv = lax.all_to_all(packed, SEQ, split_axis=0, concat_axis=0, tiled=True)
    own = stack((w_gate[0].T, w_up[0].T, w_down[0]), 0, ANY)
    across = to_core(own)
    weights = stack((own, across), 1, VMEM)
    second = gather_second(first)
    attended = attend(qkv.reshape(2048, 384))
    blocks = attended.reshape(8, 2 * T, HEAD_DIM)
    returned = lax.all_to_all(blocks, ("y", "x"), split_axis=0, concat_axis=0, tiled=True)
    pieces = [first[k] for k in FIRST] + [second[k] for k in SECOND]
    pieces += list(gather_third(second))
    order = [((y + dy) % 2) * 4 + (x + dx) % 4 for dy, dx in FIRST + SECOND + ((1, 2),)]
    place = jnp.stack(order + [c]).astype(jnp.int32)
    mine, theirs = project(place, returned, pieces)
    residual, normed = norm(mine, to_core(theirs), stream[0], norm_gain)

    first = gather_first(normed)
    first[0, 1], first[1, 0], weights = lax.optimization_barrier((first[0, 1], first[1, 0], weights))
    second = gather_second(first)
    outs = ffn([first[k] for k in FIRST], weights, [H] * (4 * SPLIT))
    outs, second = lax.optimization_barrier((outs, second))
    far = ffn(list(gather_third(second)), weights)
    far, second = lax.optimization_barrier((far, [second[k] for k in SECOND]))
    r0 = to_side(far[0])
    r1 = to_plus(far[1])
    r2 = to_minus(far[2])
    sm_, pp_, sp_ = ffn(second, weights)
    merged = merge((pp_, sp_, sm_), (r0, r1, r2))
    shares = []
    for h in range(SPLIT):
        pp_, sp_, sm_ = merged[h::SPLIT]
        shares.append((to_minus(sm_), to_plus(pp_), to_side(sp_)))
    done = []
    for h in range(SPLIT):
        t0, t1, t2 = shares[h]
        own_, m_, p_, s_ = outs[h::SPLIT]
        s_ = added(s_, t0)
        p_ = added(p_, t1, t2)
        arrived = to_minus(m_), to_plus(p_), to_side(s_)
        total = finish(h * H, residual, own_, *arrived)
        done.append(lax.ppermute(total, "s", [((i - 1) % 16, i) for i in range(16)]))
    return jnp.concatenate(done, 0)[None]


def solution(mesh):
    fine = Mesh(np.asarray(mesh.devices).reshape(16, 2, 4, 2), ("s", "y", "x", "c"))
    rows = P("s", SEQ, None)
    placed = (rows, rows, rows, rows, rows, P("s", None), P("s", None, SEQ), P("s", None, SEQ), rows)
    return jax.shard_map(layer, mesh=fine, in_specs=placed, out_specs=rows, check_vma=False)
```
